32 devices in a mesh: groups: 2 (over x), mix: 16 (over z, y, core).
Axes of the slice: x: 2, y: 2, z: 4, core: 2. Of those that a mesh axis runs over, the one named last changes fastest.
Arguments:
- recording: bfloat16 [8, 16384, 768], P('groups', 'mix'), parts along dimension 0, may hold values from -6 to 6
- mix_gain: float32 [1, 768], replicated, may hold values from 0.25 to 1.75
- block_weights: bfloat16 [1, 4, 128, 2, 128, 128], P(None, None, 'mix'), may hold values from -0.375 to 0.375
- section_perm: int32 [1, 4, 128], replicated, may hold values from 0 to 127, each once within a row
- block_mask: int32 [1, 4, 128], P(None, None, 'mix'), may hold values 0 or 1
- ffn_gain: float32 [1, 768], replicated, may hold values from 0.25 to 1.75
- ffn_in: bfloat16 [1, 2, 768, 2048], P(None, None, None, 'mix'), may hold values from -0.21875 to 0.21875
- ffn_out: bfloat16 [1, 768, 2048], P(None, None, 'mix'), may hold values from -0.125 to 0.125
Outputs:
- encoded: bfloat16 [8, 16384, 768], P('groups', 'mix'), parts along dimension 0
The draws below stay inside these ranges and needn't reach their ends.
There are 2 independent parts, one for each index of `groups`. The reference program is written for one: setup_inputs(seed, part) draws one part's arguments, and reference() takes and returns one part's arrays. A program takes and returns all parts, laid end to end along the dimension named above; an argument that names none is the same for every part. Nothing has to cross between parts.
Inputs may be any that keep to these rules, and one draw needn't show every extreme that they name: Each row section_perm[l, s] holds every number of 0 to 127 once.
All inputs are finite; a program needn't handle non-finite values. No bound on the sum of `block_mask` on one device may be relied on, other than what follows from the above.
Results may differ from the reference program's by a relative error of at most 0.013.
Values may be sent and summed in bfloat16 or wider, within the bound.
A program may use at most 192 MiB of HBM per device.

```python
import jax
import jax.numpy as jnp
from jax import lax

CH = 16384
BLK = 128
NB = 128
D = 768
FF = 2048
SECTIONS = 4
LAYERS = 1
TT = 4


def set_ends(array, own_key, smallest, top_value):
    spot = [jax.random.randint(jax.random.fold_in(own_key, axis), (), 0, length) for axis, length in enumerate(array.shape)]
    main_axis = array.shape.index(max(array.shape))
    neighbour = spot[:main_axis] + [(spot[main_axis] + 1) % array.shape[main_axis]] + spot[main_axis + 1:]
    return array.at[tuple(spot)].set(smallest).at[tuple(neighbour)].set(top_value)


def levels(rng, dims, shards, smallest, largest):
    def one(dim, parts):
        steps = jax.random.uniform(jax.random.fold_in(jax.random.fold_in(rng, 6), dim), (parts,), jnp.float32, smallest / len(shards), largest / len(shards))
        return jnp.repeat(jnp.exp(steps), dims[dim] // parts).reshape((-1,) + (1,) * (len(dims) - dim - 1))

    factor_of = one(*shards[0])
    for cut in shards[1:]:
        factor_of = factor_of * one(*cut)
    return factor_of


def normal_values(stream_key, extent, deviation, most, cuts=(), held_as=jnp.bfloat16):
    factor_of = levels(stream_key, extent, cuts, -0.22, 0.18) if cuts else 1.0
    values = jax.random.normal(stream_key, extent, jnp.float32) * deviation * factor_of
    return jnp.minimum(jnp.maximum(values, -most), most).astype(held_as)


def setup_inputs(seed: int = 0, part: int = 0) -> dict:
    keys = jax.random.split(jax.random.key(seed), 9)
    part_splits = jax.random.split(jax.random.fold_in(keys[8], part), 9)
    recording = normal_values(part_splits[0], (TT, CH, D), 1.0, 6.0, ((1, 16),))
    mix_gain = jnp.clip(1.0 + 0.15 * jax.random.normal(keys[1], (LAYERS, D), jnp.float32), 0.25, 1.75)
    block_weights = normal_values(keys[2], (LAYERS, SECTIONS, NB, 2, BLK, BLK), (2 * BLK) ** -0.5, 0.375, ((2, 16),))
    section_perm = jax.vmap(lambda own: jax.random.permutation(own, BLK))(jax.random.split(keys[3], LAYERS * SECTIONS)).reshape((LAYERS, SECTIONS, BLK)).astype(jnp.int32)
    block_mask = set_ends((jax.random.randint(keys[4], (LAYERS, SECTIONS, NB), 0, 4) < 3).astype(jnp.int32), jax.random.fold_in(keys[4], 1), 0, 1)
    ffn_gain = jnp.clip(1.0 + 0.15 * jax.random.normal(keys[5], (LAYERS, D), jnp.float32), 0.25, 1.75)
    ffn_in = normal_values(keys[6], (LAYERS, 2, D, FF), D ** -0.5, 0.21875, ((3, 16),))
    ffn_out = normal_values(keys[7], (LAYERS, D, FF), FF ** -0.5, 0.125, ((2, 16),))
    return {"recording": recording, "mix_gain": mix_gain, "block_weights": block_weights, "section_perm": section_perm, "block_mask": block_mask, "ffn_gain": ffn_gain, "ffn_in": ffn_in, "ffn_out": ffn_out}


epsilon = 1e-05

def rms_scale(values, gain):
    values = values.astype(jnp.float32)
    mean_sq = lax.optimization_barrier(jnp.mean(values * values, axis=-1, keepdims=True))
    return values * lax.rsqrt(mean_sq + epsilon) * gain

def reference(recording, mix_gain, block_weights, section_perm, block_mask, ffn_gain, ffn_in, ffn_out):
    total_bits = NB.bit_length() - 1

    def encode_token(token_frame):
        for layer_idx in range(LAYERS):
            normed = rms_scale(token_frame, mix_gain[layer_idx]).astype(jnp.bfloat16)
            blocks = normed.reshape(NB, BLK, D)
            for section_idx in range(SECTIONS):
                section_bit = total_bits - 1 - section_idx
                permuted = jnp.take(blocks, section_perm[layer_idx, section_idx], axis=1)
                partner_ids = jnp.arange(NB, dtype=jnp.int32) ^ 1 << section_bit
                partner = jnp.take(permuted, partner_ids, axis=0)
                weights = block_weights[layer_idx, section_idx].astype(jnp.float32)
                own_term = jnp.einsum('noi,nid->nod', weights[:, 0], permuted.astype(jnp.float32))
                far_term = jnp.einsum('noi,nid->nod', weights[:, 1], partner.astype(jnp.float32))
                gate_far = block_mask[layer_idx, section_idx].astype(jnp.float32)[:, None, None]
                blocks = (own_term + gate_far * far_term).astype(jnp.bfloat16)
            mixed = (token_frame.astype(jnp.float32) + blocks.reshape(CH, D).astype(jnp.float32)).astype(jnp.bfloat16)
            ffn_normed = rms_scale(mixed, ffn_gain[layer_idx]).astype(jnp.bfloat16)
            gate_proj = jnp.dot(ffn_normed, ffn_in[layer_idx, 0], preferred_element_type=jnp.float32)
            up_proj = jnp.dot(ffn_normed, ffn_in[layer_idx, 1], preferred_element_type=jnp.float32)
            hidden = (jax.nn.silu(gate_proj) * up_proj).astype(jnp.bfloat16)
            down_proj = lax.dot_general(hidden, ffn_out[layer_idx], (((1,), (1,)), ((), ())), preferred_element_type=jnp.float32)
            token_frame = (mixed.astype(jnp.float32) + down_proj).astype(jnp.bfloat16)
        return token_frame
    return lax.map(encode_token, recording)
```

```python
import functools

import jax
import jax.numpy as jnp
from jax import lax
from jax.experimental import pallas as pl
from jax.experimental.pallas import tpu as pltpu
from jax.sharding import PartitionSpec as P

epsilon = 1e-05
WINDOW = 4
RING = 4
FTILE = 512


def rms_scale(values, gain):
    values = values.astype(jnp.float32)
    mean_sq = jnp.mean(values * values, axis=-1, keepdims=True)
    return values * lax.rsqrt(mean_sq + epsilon) * gain


def mixing_kernel(
    dims,
    x_ref,
    gain1_ref,
    bw_ref,
    perm_ref,
    mask_ref,
    gain2_ref,
    wl_ref,
    out_ref,
    own0,
    ring,
    far,
    wc,
    wf,
    hn,
    acc,
    send_sem,
    recv_sem,
    ag_send,
    ag_recv,
    local_sem,
    out_sem,
):
    n_dev, sections, nb, batch, first_bit = dims
    chunks, blk, width = x_ref.shape
    hidden_units = wf.shape[1]
    shard = wl_ref.shape[1]
    n_batches = chunks // batch
    bits = n_dev.bit_length() - 1
    last = sections - 1
    me = lax.axis_index("mix")
    partners = [me + (1 << b) * (1 - 2 * ((me // (1 << b)) % 2)) for b in range(bits)]

    local = pltpu.make_async_copy(wl_ref, wf.at[:, pl.ds(0, shard), :], local_sem)
    local.start()

    barrier = pltpu.get_barrier_semaphore()
    for b in range(bits):
        pl.semaphore_signal(
            barrier, inc=1, device_id={"mix": partners[b]}, device_id_type=pl.DeviceIdType.MESH
        )
    pl.semaphore_wait(barrier, bits)

    def own_at(s, k):
        return own0.at[k] if s == 0 else ring.at[s - 1, k % RING]

    def exchange(s, k):
        return pltpu.make_async_remote_copy(
            src_ref=own_at(s, k),
            dst_ref=far.at[s, k],
            send_sem=send_sem.at[s, k],
            recv_sem=recv_sem.at[s, k],
            device_id={"mix": partners[first_bit - s]},
            device_id_type=pl.DeviceIdType.MESH,
        )

    def gather_step(g):
        count = shard << g
        return pltpu.make_async_remote_copy(
            src_ref=wf.at[:, pl.ds(0, count), :],
            dst_ref=wf.at[:, pl.ds(count, count), :],
            send_sem=ag_send.at[g],
            recv_sem=ag_recv.at[g],
            device_id={"mix": partners[bits - 1 - g]},
            device_id_type=pl.DeviceIdType.MESH,
        )

    def norm_and_send(k):
        own0[k] = rms_scale(x_ref[k], gain1_ref[...]).astype(jnp.bfloat16)
        exchange(0, k).start()

    def first(k, carry):
        norm_and_send(k)
        return carry

    window = min(WINDOW, chunks)
    lax.fori_loop(0, window, first, 0)
    if bits:
        local.wait()
        gather_step(0).start()

    def fold(q, carry):
        s = q // nb
        where_to = lax.broadcasted_iota(jnp.int32, (blk, blk), 1)
        hot = (perm_ref[s] == where_to).astype(jnp.float32).astype(jnp.bfloat16)
        keep = mask_ref[q].astype(jnp.float32)
        wc[q, :, :blk] = jnp.dot(
            bw_ref[q, 0], hot, preferred_element_type=jnp.float32
        ).astype(jnp.bfloat16)
        wc[q, :, blk:] = (
            keep * jnp.dot(bw_ref[q, 1], hot, preferred_element_type=jnp.float32)
        ).astype(jnp.bfloat16)
        return carry

    lax.fori_loop(0, sections * nb, fold, 0)

    def section(s, k):
        both = jnp.concatenate([own_at(s, k)[...], far[s, k]], axis=0)
        return jnp.dot(
            wc[s * nb + k % nb], both, preferred_element_type=jnp.float32
        ).astype(jnp.bfloat16)

    def ffn(b, carry):
        rows = batch * blk
        base = pl.multiple_of(b * batch, batch)
        mixed = own0[pl.ds(base, batch)].reshape(rows, width)
        hn[...] = rms_scale(mixed, gain2_ref[...]).astype(jnp.bfloat16)
        acc[...] = mixed.astype(jnp.float32)

        def tile(f, inner):
            at = pl.ds(pl.multiple_of(f * FTILE, FTILE), FTILE)
            nt = (((1,), (1,)), ((), ()))
            gate = lax.dot_general(hn[...], wf[0, at, :], nt, preferred_element_type=jnp.float32)
            up = lax.dot_general(hn[...], wf[1, at, :], nt, preferred_element_type=jnp.float32)
            hidden = (gate / (1.0 + jnp.exp(-gate)) * up).astype(jnp.bfloat16)
            acc[...] += jnp.dot(hidden, wf[2, at, :], preferred_element_type=jnp.float32)
            return inner

        lax.fori_loop(0, hidden_units // FTILE, tile, 0)
        own0[pl.ds(base, batch)] = acc[...].astype(jnp.bfloat16).reshape(batch, blk, width)
        pltpu.make_async_copy(
            own0.at[pl.ds(base, batch)], out_ref.at[pl.ds(base, batch)], out_sem.at[b]
        ).start()
        return carry

    ffn_from = chunks // 2 + 1
    gather_at = [1 + g * (ffn_from - 1) // max(bits, 1) for g in range(bits)]

    def ready(i):
        done = jnp.clip((i - last + 1) // batch, 0, n_batches)
        return jnp.where(i >= ffn_from, done, 0)

    def step(i, carry):
        for g in range(1, bits):

            @pl.when(i == gather_at[g])
            def _(g=g):
                gather_step(g - 1).wait_recv()
                gather_step(g).start()

        @pl.when(i + window < chunks)
        def _():
            norm_and_send(i + window)

        for s in range(sections):
            k = i - s

            @pl.when(jnp.logical_and(k >= 0, k < chunks))
            def _(s=s, k=k):
                exchange(s, k).wait_recv()
                result = section(s, k)
                if s < last:

                    @pl.when(k >= RING)
                    def _():
                        exchange(s + 1, k - RING).wait_send()

                    own_at(s + 1, k)[...] = result
                    exchange(s + 1, k).start()
                else:
                    exchange(0, k).wait_send()
                    own0[k] = (
                        x_ref[k].astype(jnp.float32) + result.astype(jnp.float32)
                    ).astype(jnp.bfloat16)

        if bits:

            @pl.when(i == ffn_from)
            def _():
                gather_step(bits - 1).wait_recv()

        lax.fori_loop(ready(i - 1), ready(i), ffn, 0)
        return carry

    lax.fori_loop(0, chunks + last, step, 0)

    for s in range(1, sections):
        for k in range(max(chunks - RING, 0), chunks):
            exchange(s, k).wait_send()
    for g in range(bits):
        gather_step(g).wait_send()
    for b in range(n_batches):
        at = pl.ds(b * batch, batch)
        pltpu.make_async_copy(own0.at[at], out_ref.at[at], out_sem.at[b]).wait()


def on_device(
    recording, mix_gain, block_weights, section_perm, block_mask, ffn_gain, ffn_in, ffn_out
):
    time_steps, local_ch, width = recording.shape
    sections, nb, _, blk, _ = block_weights.shape[1:]
    n_dev = lax.axis_size("mix")
    chunks = time_steps * nb
    batch = 4
    while chunks % batch:
        batch //= 2
    bits = n_dev.bit_length() - 1
    total_bits = (n_dev * nb).bit_length() - 1
    first_bit = total_bits - 1 - (nb.bit_length() - 1)
    shard = ffn_in.shape[-1]
    local_weights = jnp.concatenate(
        [jnp.swapaxes(ffn_in[0], 1, 2), jnp.swapaxes(ffn_out, 1, 2)], axis=0
    )
    vmem = pl.BlockSpec(memory_space=pltpu.VMEM)
    anywhere = pl.BlockSpec(memory_space=pl.ANY)
    result = pl.pallas_call(
        functools.partial(mixing_kernel, (n_dev, sections, nb, batch, first_bit)),
        out_shape=jax.ShapeDtypeStruct((chunks, blk, width), jnp.bfloat16),
        in_specs=[vmem, vmem, vmem, vmem, pl.BlockSpec(memory_space=pltpu.SMEM), vmem, anywhere],
        out_specs=anywhere,
        scratch_shapes=[
            pltpu.VMEM((chunks, blk, width), jnp.bfloat16),
            pltpu.VMEM((sections - 1, RING, blk, width), jnp.bfloat16),
            pltpu.VMEM((sections, chunks, blk, width), jnp.bfloat16),
            pltpu.VMEM((sections * nb, blk, 2 * blk), jnp.bfloat16),
            pltpu.VMEM((3, shard * n_dev, width), jnp.bfloat16),
            pltpu.VMEM((batch * blk, width), jnp.bfloat16),
            pltpu.VMEM((batch * blk, width), jnp.float32),
            pltpu.SemaphoreType.DMA((sections, chunks)),
            pltpu.SemaphoreType.DMA((sections, chunks)),
            pltpu.SemaphoreType.DMA((bits,)),
            pltpu.SemaphoreType.DMA((bits,)),
            pltpu.SemaphoreType.DMA,
            pltpu.SemaphoreType.DMA((chunks // batch,)),
        ],
        compiler_params=pltpu.CompilerParams(
            collective_id=0, has_side_effects=True, vmem_limit_bytes=60 * 1024 * 1024
        ),
    )(
        recording.reshape(chunks, blk, width),
        mix_gain,
        block_weights[0].reshape(sections * nb, 2, blk, blk),
        section_perm[0][:, :, None],
        block_mask[0].reshape(sections * nb),
        ffn_gain,
        local_weights,
    )
    return result.reshape(time_steps, local_ch, width)


def solution(mesh):
    in_specs = (
        P("groups", "mix", None),
        P(),
        P(None, None, "mix", None, None, None),
        P(),
        P(None, None, "mix"),
        P(),
        P(None, None, None, "mix"),
        P(None, None, "mix"),
    )
    out_specs = P("groups", "mix", None)
    return jax.shard_map(
        on_device, mesh=mesh, in_specs=in_specs, out_specs=out_specs, check_vma=False
    )
```

```python
import functools

import jax
import jax.numpy as jnp
from jax import lax
from jax.experimental import pallas as pl
from jax.experimental.pallas import tpu as pltpu
from jax.sharding import PartitionSpec as P

epsilon = 1e-05
WINDOW = 4
LAG = 4
RING = 8
FTILE = 512


def rms_scale(values, gain):
    values = values.astype(jnp.float32)
    mean_sq = jnp.mean(values * values, axis=-1, keepdims=True)
    return values * lax.rsqrt(mean_sq + epsilon) * gain


def mixing_kernel(
    dims,
    x_ref,
    gain1_ref,
    bw_ref,
    perm_ref,
    mask_ref,
    gain2_ref,
    wl_ref,
    out_ref,
    own0,
    ring,
    far,
    wc,
    wf,
    hn,
    acc,
    send_sem,
    recv_sem,
    ag_send,
    ag_recv,
    local_sem,
    out_sem,
):
    n_dev, sections, nb, batch, first_bit, split = dims
    chunks, blk, width = x_ref.shape
    hidden_units = wf.shape[1]
    shard = wl_ref.shape[1] // split
    n_batches = chunks // batch
    bits = n_dev.bit_length() - 1
    last = sections - 1
    me = lax.axis_index("mix")
    partners = [me + (1 << b) * (1 - 2 * ((me // (1 << b)) % 2)) for b in range(bits)]

    group = lax.axis_index("groups")
    sibling = group + 1 - 2 * (group % 2)
    targets = [{"mix": partners[b]} for b in range(bits)]
    if split == 2:
        targets = targets + [{"groups": sibling}]
    piece = pl.ds(pl.multiple_of((group % split) * shard, shard), shard)
    local = pltpu.make_async_copy(
        wl_ref.at[:, piece, :], wf.at[:, pl.ds(0, shard), :], local_sem
    )
    local.start()
    route = [targets[b] for b in range(bits - 1, 0, -1)] + targets[bits:] + targets[: min(bits, 1)]
    rounds = len(route)

    barrier = pltpu.get_barrier_semaphore()
    for target in targets:
        pl.semaphore_signal(
            barrier, inc=1, device_id=target, device_id_type=pl.DeviceIdType.MESH
        )
    pl.semaphore_wait(barrier, len(targets))

    def own_at(s, k):
        return own0.at[k] if s == 0 else ring.at[s - 1, k % RING]

    def exchange(s, k):
        return pltpu.make_async_remote_copy(
            src_ref=own_at(s, k),
            dst_ref=far.at[s, k],
            send_sem=send_sem.at[s, k],
            recv_sem=recv_sem.at[s, k],
            device_id={"mix": partners[first_bit - s]},
            device_id_type=pl.DeviceIdType.MESH,
        )

    def gather_step(g):
        count = shard << g
        return pltpu.make_async_remote_copy(
            src_ref=wf.at[:, pl.ds(0, count), :],
            dst_ref=wf.at[:, pl.ds(count, count), :],
            send_sem=ag_send.at[g],
            recv_sem=ag_recv.at[g],
            device_id=route[g],
            device_id_type=pl.DeviceIdType.MESH,
        )

    def norm_and_send(k):
        own0[k] = rms_scale(x_ref[k], gain1_ref[...]).astype(jnp.bfloat16)
        exchange(0, k).start()

    def first(k, carry):
        norm_and_send(k)
        return carry

    window = min(WINDOW, chunks)
    lax.fori_loop(0, window, first, 0)
    local.wait()
    if rounds:
        gather_step(0).start()

    def fold(q, carry):
        s = q // nb
        where_to = lax.broadcasted_iota(jnp.int32, (blk, blk), 1)
        hot = (perm_ref[s] == where_to).astype(jnp.float32).astype(jnp.bfloat16)
        keep = mask_ref[q].astype(jnp.float32)
        wc[q, :, :blk] = jnp.dot(
            bw_ref[q, 0], hot, preferred_element_type=jnp.float32
        ).astype(jnp.bfloat16)
        wc[q, :, blk:] = (
            keep * jnp.dot(bw_ref[q, 1], hot, preferred_element_type=jnp.float32)
        ).astype(jnp.bfloat16)
        return carry

    lax.fori_loop(0, sections * nb, fold, 0)

    def section(s, k):
        both = jnp.concatenate([own_at(s, k)[...], far[s, k]], axis=0)
        return jnp.dot(
            wc[s * nb + k % nb], both, preferred_element_type=jnp.float32
        ).astype(jnp.bfloat16)

    def ffn(b, carry):
        rows = batch * blk
        base = pl.multiple_of(b * batch, batch)
        mixed = own0[pl.ds(base, batch)].reshape(rows, width)
        hn[...] = rms_scale(mixed, gain2_ref[...]).astype(jnp.bfloat16)
        acc[...] = mixed.astype(jnp.float32)

        def tile(f, inner):
            at = pl.ds(pl.multiple_of(f * FTILE, FTILE), FTILE)
            nt = (((1,), (1,)), ((), ()))
            gate = lax.dot_general(hn[...], wf[0, at, :], nt, preferred_element_type=jnp.float32)
            up = lax.dot_general(hn[...], wf[1, at, :], nt, preferred_element_type=jnp.float32)
            hidden = (gate / (1.0 + jnp.exp(-gate)) * up).astype(jnp.bfloat16)
            acc[...] += jnp.dot(hidden, wf[2, at, :], preferred_element_type=jnp.float32)
            return inner

        lax.fori_loop(0, hidden_units // FTILE, tile, 0)
        own0[pl.ds(base, batch)] = acc[...].astype(jnp.bfloat16).reshape(batch, blk, width)
        pltpu.make_async_copy(
            own0.at[pl.ds(base, batch)], out_ref.at[pl.ds(base, batch)], out_sem.at[b]
        ).start()
        return carry

    ffn_from = chunks // 2 + 1
    gather_at = [1 + g * (ffn_from - 1) // max(rounds, 1) for g in range(rounds)]

    def ready(i):
        done = jnp.clip((i - last * LAG + 1) // batch, 0, n_batches)
        return jnp.where(i >= ffn_from, done, 0)

    def step(i, carry):
        for g in range(1, rounds):

            @pl.when(i == gather_at[g])
            def _(g=g):
                gather_step(g - 1).wait_recv()
                gather_step(g).start()

        @pl.when(i + window < chunks)
        def _():
            norm_and_send(i + window)

        for s in range(sections):
            k = i - s * LAG

            @pl.when(jnp.logical_and(k >= 0, k < chunks))
            def _(s=s, k=k):
                exchange(s, k).wait_recv()
                result = section(s, k)
                if s < last:

                    @pl.when(k >= RING)
                    def _():
                        exchange(s + 1, k - RING).wait_send()

                    own_at(s + 1, k)[...] = result
                    exchange(s + 1, k).start()
                else:
                    exchange(0, k).wait_send()
                    own0[k] = (
                        x_ref[k].astype(jnp.float32) + result.astype(jnp.float32)
                    ).astype(jnp.bfloat16)

        if rounds:

            @pl.when(i == ffn_from)
            def _():
                gather_step(rounds - 1).wait_recv()

        lax.fori_loop(ready(i - 1), ready(i), ffn, 0)
        return carry

    lax.fori_loop(0, chunks + last * LAG, step, 0)

    for s in range(1, sections):
        for k in range(max(chunks - RING, 0), chunks):
            exchange(s, k).wait_send()
    for g in range(rounds):
        gather_step(g).wait_send()
    for b in range(n_batches):
        at = pl.ds(b * batch, batch)
        pltpu.make_async_copy(own0.at[at], out_ref.at[at], out_sem.at[b]).wait()


def on_device(
    recording, mix_gain, block_weights, section_perm, block_mask, ffn_gain, ffn_in, ffn_out
):
    time_steps, local_ch, width = recording.shape
    sections, nb, _, blk, _ = block_weights.shape[1:]
    n_dev = lax.axis_size("mix")
    chunks = time_steps * nb
    batch = 4
    while chunks % batch:
        batch //= 2
    bits = n_dev.bit_length() - 1
    total_bits = (n_dev * nb).bit_length() - 1
    first_bit = total_bits - 1 - (nb.bit_length() - 1)
    shard = ffn_in.shape[-1]
    split = 2 if lax.axis_size("groups") % 2 == 0 and shard % 32 == 0 else 1
    rounds = bits + split - 1
    local_weights = jnp.concatenate(
        [jnp.swapaxes(ffn_in[0], 1, 2), jnp.swapaxes(ffn_out, 1, 2)], axis=0
    )
    vmem = pl.BlockSpec(memory_space=pltpu.VMEM)
    anywhere = pl.BlockSpec(memory_space=pl.ANY)
    result = pl.pallas_call(
        functools.partial(mixing_kernel, (n_dev, sections, nb, batch, first_bit, split)),
        out_shape=jax.ShapeDtypeStruct((chunks, blk, width), jnp.bfloat16),
        in_specs=[vmem, vmem, vmem, vmem, pl.BlockSpec(memory_space=pltpu.SMEM), vmem, anywhere],
        out_specs=anywhere,
        scratch_shapes=[
            pltpu.VMEM((chunks, blk, width), jnp.bfloat16),
            pltpu.VMEM((sections - 1, RING, blk, width), jnp.bfloat16),
            pltpu.VMEM((sections, chunks, blk, width), jnp.bfloat16),
            pltpu.VMEM((sections * nb, blk, 2 * blk), jnp.bfloat16),
            pltpu.VMEM((3, shard * n_dev, width), jnp.bfloat16),
            pltpu.VMEM((batch * blk, width), jnp.bfloat16),
            pltpu.VMEM((batch * blk, width), jnp.float32),
            pltpu.SemaphoreType.DMA((sections, chunks)),
            pltpu.SemaphoreType.DMA((sections, chunks)),
            pltpu.SemaphoreType.DMA((rounds,)),
            pltpu.SemaphoreType.DMA((rounds,)),
            pltpu.SemaphoreType.DMA,
            pltpu.SemaphoreType.DMA((chunks // batch,)),
        ],
        compiler_params=pltpu.CompilerParams(
            collective_id=0, has_side_effects=True, vmem_limit_bytes=60 * 1024 * 1024
        ),
    )(
        recording.reshape(chunks, blk, width),
        mix_gain,
        block_weights[0].reshape(sections * nb, 2, blk, blk),
        section_perm[0][:, :, None],
        block_mask[0].reshape(sections * nb),
        ffn_gain,
        local_weights,
    )
    return result.reshape(time_steps, local_ch, width)


def solution(mesh):
    in_specs = (
        P("groups", "mix", None),
        P(),
        P(None, None, "mix", None, None, None),
        P(),
        P(None, None, "mix"),
        P(),
        P(None, None, None, "mix"),
        P(None, None, "mix"),
    )
    out_specs = P("groups", "mix", None)
    return jax.shard_map(
        on_device, mesh=mesh, in_specs=in_specs, out_specs=out_specs, check_vma=False
    )
```

```python
import functools

import jax
import jax.numpy as jnp
from jax import lax
from jax.experimental import pallas as pl
from jax.experimental.pallas import tpu as pltpu
from jax.sharding import PartitionSpec as P

epsilon = 1e-05
WINDOW = 4
OFFSETS = (0, 4, 7, 9)
RING = 8
FTILE = 512


def rms_scale(values, gain):
    values = values.astype(jnp.float32)
    mean_sq = jnp.mean(values * values, axis=-1, keepdims=True)
    return values * lax.rsqrt(mean_sq + epsilon) * gain


def mixing_kernel(
    dims,
    x_ref,
    gain1_ref,
    bw_ref,
    perm_ref,
    mask_ref,
    gain2_ref,
    wl_ref,
    out_ref,
    own0,
    ring,
    far,
    wc,
    wf,
    hn,
    acc,
    send_sem,
    recv_sem,
    ag_send,
    ag_recv,
    local_sem,
    out_sem,
):
    n_dev, sections, nb, batch, first_bit, split = dims
    chunks, blk, width = x_ref.shape
    hidden_units = wf.shape[1]
    shard = wl_ref.shape[1] // split
    n_batches = chunks // batch
    bits = n_dev.bit_length() - 1
    last = sections - 1
    me = lax.axis_index("mix")
    partners = [me + (1 << b) * (1 - 2 * ((me // (1 << b)) % 2)) for b in range(bits)]

    group = lax.axis_index("groups")
    sibling = group + 1 - 2 * (group % 2)
    targets = [{"mix": partners[b]} for b in range(bits)]
    if split == 2:
        targets = targets + [{"groups": sibling}]
    piece = pl.ds(pl.multiple_of((group % split) * shard, shard), shard)
    local = pltpu.make_async_copy(
        wl_ref.at[:, piece, :], wf.at[:, pl.ds(0, shard), :], local_sem
    )
    local.start()
    route = [targets[b] for b in range(bits - 1, 0, -1)] + targets[bits:] + targets[: min(bits, 1)]
    rounds = len(route)

    barrier = pltpu.get_barrier_semaphore()
    for target in targets:
        pl.semaphore_signal(
            barrier, inc=1, device_id=target, device_id_type=pl.DeviceIdType.MESH
        )
    pl.semaphore_wait(barrier, len(targets))

    def own_at(s, k):
        return own0.at[k] if s == 0 else ring.at[s - 1, k % RING]

    def exchange(s, k):
        return pltpu.make_async_remote_copy(
            src_ref=own_at(s, k),
            dst_ref=far.at[s, k],
            send_sem=send_sem.at[s, k],
            recv_sem=recv_sem.at[s, k],
            device_id={"mix": partners[first_bit - s]},
            device_id_type=pl.DeviceIdType.MESH,
        )

    def gather_step(g):
        count = shard << g
        return pltpu.make_async_remote_copy(
            src_ref=wf.at[:, pl.ds(0, count), :],
            dst_ref=wf.at[:, pl.ds(count, count), :],
            send_sem=ag_send.at[g],
            recv_sem=ag_recv.at[g],
            device_id=route[g],
            device_id_type=pl.DeviceIdType.MESH,
        )

    def norm_and_send(k):
        own0[k] = rms_scale(x_ref[k], gain1_ref[...]).astype(jnp.bfloat16)
        exchange(0, k).start()

    def first(k, carry):
        norm_and_send(k)
        return carry

    window = min(WINDOW, chunks)
    lax.fori_loop(0, window, first, 0)
    local.wait()
    if rounds:
        gather_step(0).start()

    def fold(q, carry):
        s = q // nb
        where_to = lax.broadcasted_iota(jnp.int32, (blk, blk), 1)
        hot = (perm_ref[s] == where_to).astype(jnp.float32).astype(jnp.bfloat16)
        keep = mask_ref[q].astype(jnp.float32)
        wc[q, :, :blk] = jnp.dot(
            bw_ref[q, 0], hot, preferred_element_type=jnp.float32
        ).astype(jnp.bfloat16)
        wc[q, :, blk:] = (
            keep * jnp.dot(bw_ref[q, 1], hot, preferred_element_type=jnp.float32)
        ).astype(jnp.bfloat16)
        return carry

    lax.fori_loop(0, sections * nb, fold, 0)

    def section(s, k):
        both = jnp.concatenate([own_at(s, k)[...], far[s, k]], axis=0)
        return jnp.dot(
            wc[s * nb + k % nb], both, preferred_element_type=jnp.float32
        ).astype(jnp.bfloat16)

    def ffn(b, carry):
        rows = batch * blk
        base = pl.multiple_of(b * batch, batch)
        mixed = own0[pl.ds(base, batch)].reshape(rows, width)
        hn[...] = rms_scale(mixed, gain2_ref[...]).astype(jnp.bfloat16)
        acc[...] = mixed.astype(jnp.float32)

        def tile(f, inner):
            at = pl.ds(pl.multiple_of(f * FTILE, FTILE), FTILE)
            nt = (((1,), (1,)), ((), ()))
            gate = lax.dot_general(hn[...], wf[0, at, :], nt, preferred_element_type=jnp.float32)
            up = lax.dot_general(hn[...], wf[1, at, :], nt, preferred_element_type=jnp.float32)
            hidden = (gate / (1.0 + jnp.exp(-gate)) * up).astype(jnp.bfloat16)
            acc[...] += jnp.dot(hidden, wf[2, at, :], preferred_element_type=jnp.float32)
            return inner

        lax.fori_loop(0, hidden_units // FTILE, tile, 0)
        own0[pl.ds(base, batch)] = acc[...].astype(jnp.bfloat16).reshape(batch, blk, width)
        pltpu.make_async_copy(
            own0.at[pl.ds(base, batch)], out_ref.at[pl.ds(base, batch)], out_sem.at[b]
        ).start()
        return carry

    ffn_from = 5 * chunks // 8 + 1
    gather_at = [1 + g * (ffn_from - 1) // max(rounds, 1) for g in range(rounds)]

    def ready(i):
        done = jnp.clip((i - OFFSETS[last] + 1) // batch, 0, n_batches)
        return jnp.where(i >= ffn_from, done, 0)

    def step(i, carry):
        for g in range(1, rounds):

            @pl.when(i == gather_at[g])
            def _(g=g):
                gather_step(g - 1).wait_recv()
                gather_step(g).start()

        @pl.when(i + window < chunks)
        def _():
            norm_and_send(i + window)

        for s in range(sections):
            k = i - OFFSETS[s]

            @pl.when(jnp.logical_and(k >= 0, k < chunks))
            def _(s=s, k=k):
                exchange(s, k).wait_recv()
                result = section(s, k)
                if s < last:

                    @pl.when(k >= RING)
                    def _():
                        exchange(s + 1, k - RING).wait_send()

                    own_at(s + 1, k)[...] = result
                    exchange(s + 1, k).start()
                else:
                    exchange(0, k).wait_send()
                    own0[k] = (
                        x_ref[k].astype(jnp.float32) + result.astype(jnp.float32)
                    ).astype(jnp.bfloat16)

        if rounds:

            @pl.when(i == ffn_from)
            def _():
                gather_step(rounds - 1).wait_recv()

        lax.fori_loop(ready(i - 1), ready(i), ffn, 0)
        return carry

    lax.fori_loop(0, chunks + OFFSETS[last], step, 0)

    for s in range(1, sections):
        for k in range(max(chunks - RING, 0), chunks):
            exchange(s, k).wait_send()
    for g in range(rounds):
        gather_step(g).wait_send()
    for b in range(n_batches):
        at = pl.ds(b * batch, batch)
        pltpu.make_async_copy(own0.at[at], out_ref.at[at], out_sem.at[b]).wait()


def on_device(
    recording, mix_gain, block_weights, section_perm, block_mask, ffn_gain, ffn_in, ffn_out
):
    time_steps, local_ch, width = recording.shape
    sections, nb, _, blk, _ = block_weights.shape[1:]
    n_dev = lax.axis_size("mix")
    chunks = time_steps * nb
    batch = 4
    while chunks % batch:
        batch //= 2
    bits = n_dev.bit_length() - 1
    total_bits = (n_dev * nb).bit_length() - 1
    first_bit = total_bits - 1 - (nb.bit_length() - 1)
    shard = ffn_in.shape[-1]
    split = 2 if lax.axis_size("groups") % 2 == 0 and shard % 32 == 0 else 1
    rounds = bits + split - 1
    local_weights = jnp.concatenate(
        [jnp.swapaxes(ffn_in[0], 1, 2), jnp.swapaxes(ffn_out, 1, 2)], axis=0
    )
    vmem = pl.BlockSpec(memory_space=pltpu.VMEM)
    anywhere = pl.BlockSpec(memory_space=pl.ANY)
    result = pl.pallas_call(
        functools.partial(mixing_kernel, (n_dev, sections, nb, batch, first_bit, split)),
        out_shape=jax.ShapeDtypeStruct((chunks, blk, width), jnp.bfloat16),
        in_specs=[vmem, vmem, vmem, vmem, pl.BlockSpec(memory_space=pltpu.SMEM), vmem, anywhere],
        out_specs=anywhere,
        scratch_shapes=[
            pltpu.VMEM((chunks, blk, width), jnp.bfloat16),
            pltpu.VMEM((sections - 1, RING, blk, width), jnp.bfloat16),
            pltpu.VMEM((sections, chunks, blk, width), jnp.bfloat16),
            pltpu.VMEM((sections * nb, blk, 2 * blk), jnp.bfloat16),
            pltpu.VMEM((3, shard * n_dev, width), jnp.bfloat16),
            pltpu.VMEM((batch * blk, width), jnp.bfloat16),
            pltpu.VMEM((batch * blk, width), jnp.float32),
            pltpu.SemaphoreType.DMA((sections, chunks)),
            pltpu.SemaphoreType.DMA((sections, chunks)),
            pltpu.SemaphoreType.DMA((rounds,)),
            pltpu.SemaphoreType.DMA((rounds,)),
            pltpu.SemaphoreType.DMA,
            pltpu.SemaphoreType.DMA((chunks // batch,)),
        ],
        compiler_params=pltpu.CompilerParams(
            collective_id=0, has_side_effects=True, vmem_limit_bytes=60 * 1024 * 1024
        ),
    )(
        recording.reshape(chunks, blk, width),
        mix_gain,
        block_weights[0].reshape(sections * nb, 2, blk, blk),
        section_perm[0][:, :, None],
        block_mask[0].reshape(sections * nb),
        ffn_gain,
        local_weights,
    )
    return result.reshape(time_steps, local_ch, width)


def solution(mesh):
    in_specs = (
        P("groups", "mix", None),
        P(),
        P(None, None, "mix", None, None, None),
        P(),
        P(None, None, "mix"),
        P(),
        P(None, None, None, "mix"),
        P(None, None, "mix"),
    )
    out_specs = P("groups", "mix", None)
    return jax.shard_map(
        on_device, mesh=mesh, in_specs=in_specs, out_specs=out_specs, check_vma=False
    )
```
